32 devices in a mesh: box: 2 (over x), gx: 16 (over z, y, core).
Axes of the slice: x: 2, y: 2, z: 4, core: 2. Of those that a mesh axis runs over, the one named last changes fastest.
Arguments:
- atom_frac: float32 [3, 64, 128], P(None, ('box', 'gx')), parts along dimension 1, may hold values from 0 to 1
- atom_charge: float32 [4, 64, 128], P(None, ('box', 'gx')), parts along dimension 1, may hold values from -6 to 6
- cell_x: int32 [64, 128], P(('box', 'gx')), parts along dimension 0, may hold values from 0 to 15
- cell_y: int32 [64, 128], P(('box', 'gx')), parts along dimension 0, may hold values from 2 to 60
- cell_z: int32 [64, 128], P(('box', 'gx')), parts along dimension 0, may hold values from 0 to 255
- tile_count: int32 [64], P(('box', 'gx')), parts along dimension 0, may hold values from 64 to 128
- tile_offset: int32 [64], P(('box', 'gx')), parts along dimension 0, may hold values from 0 to 255
- live_tiles: int32 [32], P(('box', 'gx')), parts along dimension 0, may hold values from 1 to 2, as said below
Outputs:
- charge_grad: float32 [4, 64, 128], P(None, ('box', 'gx')), parts along dimension 1
- forces: float32 [3, 64, 128], P(None, ('box', 'gx')), parts along dimension 1
- potential: float32 [4, 512, 256, 256], P(None, ('box', 'gx')), parts along dimension 1
The draws below stay inside these ranges and needn't reach their ends.
There are 2 independent parts, one for each index of `box`. The reference program is written for one: setup_inputs(seed, part) draws one part's arguments, and reference() takes and returns one part's arrays. A program takes and returns all parts, laid end to end along the dimension named above; each array names one. Nothing has to cross between parts.
Inputs may be any that keep to these rules, and one draw needn't show every extreme that they name: `live_tiles`: slots at or beyond an index's live count hold no atoms; in every draw some indices have all 2 slots in use. `cell_y`: an atom's six cells along the second dimension lie within its tile's block of 64 rows.
All inputs are finite; a program needn't handle non-finite values.
Results may differ from the reference program's by a relative error of at most 0.0003.
Values sent between devices are 32-bit elements; how exact they have to be, the bound alone decides.
No kernel may reach another device: no remote copies, remote signals or barrier semaphores. Data moves between devices by JAX's collectives and lax.ppermute only.
A program may use at most 256 MiB of HBM per device.

```python
import math
import jax
import jax.numpy as jnp
from jax import lax

CH = 4
MX = 256
MY = 256
MZ = 256
TILE = 128
WIN = 64
SLOTS = 2
PLANES = 16
TILES = 32
N_GX = 16


def draw_live_tiles(key, part):
    first_key = jax.random.fold_in(key, 11)
    second_key = jax.random.fold_in(key, 12)
    lowest = max(1, SLOTS // 4)
    upper_bound = max(lowest + 1, SLOTS // 2 + 1)
    base_loads = jax.random.randint(first_key, (N_GX,), lowest, upper_bound)
    band_start = jax.random.randint(second_key, (), 0, N_GX)
    positions = jnp.arange(N_GX)
    in_band = jnp.remainder(positions - band_start, N_GX) < max(1, N_GX // 8)
    return jnp.where(in_band, SLOTS, base_loads).astype(jnp.int32)


def with_ends(result, stream_key, least, top_value):
    extent = result.shape
    spot = [jax.random.randint(jax.random.fold_in(stream_key, axis), (), 0, extent[axis]) for axis in range(len(extent))]
    result = result.at[tuple(spot)].set(least)
    longest = extent.index(max(extent))
    spot[longest] = (spot[longest] + 1) % extent[longest]
    return result.at[tuple(spot)].set(top_value)


def steps_of(stream_key, shape, cuts, smallest, largest):
    def one(position, shards_of):
        heights = jax.random.uniform(jax.random.fold_in(jax.random.fold_in(stream_key, 6), position), (shards_of,), jnp.float32, smallest / len(cuts), largest / len(cuts))
        return jnp.repeat(jnp.exp(heights), shape[position] // shards_of).reshape((-1,) + (1,) * (len(shape) - position - 1))

    loudness = one(*cuts[0])
    for cut in cuts[1:]:
        loudness = loudness * one(*cut)
    return loudness


def bell_draw(key, extent, spread, reach, pieces=(), held_as=jnp.bfloat16):
    factor_of = steps_of(key, extent, pieces, -0.22, 0.18) if pieces else 1.0
    drawn = jax.random.normal(key, extent, jnp.float32) * spread * factor_of
    return jnp.minimum(jnp.maximum(drawn, -reach), reach).astype(held_as)


def setup_inputs(seed: int = 0, part: int = 0) -> dict:
    key_of = jax.random.split(jax.random.key(seed), 9)
    part_keys = jax.random.split(jax.random.fold_in(key_of[8], part), 9)
    return {
        "atom_frac": jnp.clip(1.0 * jax.random.uniform(part_keys[0], (3, TILES, TILE), jnp.float32) ** steps_of(part_keys[0], (3, TILES, TILE), ((1, 16),), -0.2, 0.2), 0.0, 1.0),
        "atom_charge": bell_draw(part_keys[1], (CH, TILES, TILE), 1.0, 6.0, ((1, 16),), jnp.float32),
        "cell_x": with_ends(jax.random.randint(part_keys[2], (TILES, TILE), 0, PLANES), jax.random.fold_in(part_keys[2], 1), 0, PLANES - 1).astype(jnp.int32),
        "cell_y": with_ends(jax.random.randint(part_keys[3], (TILES, TILE), 2, WIN - 3), jax.random.fold_in(part_keys[3], 1), 2, (WIN - 3) - 1).astype(jnp.int32),
        "cell_z": with_ends(jax.random.randint(part_keys[4], (TILES, TILE), 0, MZ), jax.random.fold_in(part_keys[4], 1), 0, MZ - 1).astype(jnp.int32),
        "tile_count": with_ends(jax.random.randint(part_keys[5], (TILES,), TILE // 2, TILE + 1), jax.random.fold_in(part_keys[5], 1), TILE // 2, TILE).astype(jnp.int32),
        "tile_offset": with_ends(jax.random.randint(part_keys[6], (TILES,), 0, MY), jax.random.fold_in(part_keys[6], 1), 0, MY - 1).astype(jnp.int32),
        "live_tiles": draw_live_tiles(jax.random.fold_in(jax.random.fold_in(key_of[8], part), 71), part),
    }


SMEARING = 0.7
COULOMB = 8.0


def spline_weights(fraction):
    t1 = fraction
    t2 = t1 * t1
    t3 = t2 * t1
    t4 = t3 * t1
    t5 = t4 * t1
    rest = 1.0 - t1
    weights = jnp.stack([rest ** 5, 26.0 - 50.0 * t1 + 20.0 * t2 + 20.0 * t3 - 20.0 * t4 + 5.0 * t5, 66.0 - 60.0 * t2 + 30.0 * t4 - 10.0 * t5, 26.0 + 50.0 * t1 + 20.0 * t2 - 20.0 * t3 - 20.0 * t4 + 10.0 * t5, 1.0 + 5.0 * t1 + 10.0 * t2 + 10.0 * t3 + 5.0 * t4 - 5.0 * t5, t5]) / 120.0
    slopes = jnp.stack([-5.0 * rest ** 4, -50.0 + 40.0 * t1 + 60.0 * t2 - 80.0 * t3 + 25.0 * t4, -120.0 * t1 + 120.0 * t3 - 50.0 * t4, 50.0 + 40.0 * t1 - 60.0 * t2 - 80.0 * t3 + 50.0 * t4, 5.0 + 20.0 * t1 + 30.0 * t2 + 20.0 * t3 - 25.0 * t4, 5.0 * t4]) / 120.0
    return weights, slopes


def axis_weights(fraction, anchor, cells, modulus):
    offsets = jnp.remainder(cells[:, None] - anchor[None, :] + 2, modulus)
    weights, slopes = spline_weights(fraction)
    picks = (offsets[None, :, :] == jnp.arange(6, dtype=jnp.int32)[:, None, None]).astype(fraction.dtype)
    return jnp.sum(picks * weights[:, None, :], axis=0), jnp.sum(picks * slopes[:, None, :], axis=0)


def tile_factors(fraction, plane_cell, row_cell, column_cell, planes):
    plane_pair = axis_weights(fraction[0], plane_cell, planes, MX)
    row_pair = axis_weights(fraction[1], row_cell, jnp.arange(WIN, dtype=jnp.int32), MY)
    column_pair = axis_weights(fraction[2], column_cell, jnp.arange(MZ, dtype=jnp.int32), MZ)
    return plane_pair, row_pair, column_pair


def spread_window(masked_charge, plane_pair, row_pair, column_pair):
    product = masked_charge[:, None, None, :] * plane_pair[0][None, :, None, :] * row_pair[0][None, None, :, :]
    return jnp.einsum('cpya,za->cpyz', product, column_pair[0], precision=lax.Precision.HIGHEST)


def gather_window(window, charge, row_mask, plane_pair, row_pair, column_pair):
    stacked = jnp.stack([column_pair[0], column_pair[1]])
    paired = jnp.einsum('cpyz,kza->kcpya', window, stacked, precision=lax.Precision.HIGHEST)
    row_sum = jnp.sum(paired[0] * row_pair[0][None, None], axis=2)
    row_diff = jnp.sum(paired[0] * row_pair[1][None, None], axis=2)
    depth_diff = jnp.sum(paired[1] * row_pair[0][None, None], axis=2)
    values = jnp.sum(row_sum * plane_pair[0][None], axis=1)
    grads = jnp.stack([jnp.sum(row_sum * plane_pair[1][None], axis=1), jnp.sum(row_diff * plane_pair[0][None], axis=1), jnp.sum(depth_diff * plane_pair[0][None], axis=1)])
    slopes = jnp.sum(grads * charge[None], axis=1)
    return values * row_mask[None], slopes * row_mask[None]


def wave_terms(index, count, dtype):
    signed = jnp.where(index < count // 2, index, index - count)
    number = (2.0 * math.pi / count) * signed.astype(dtype)
    smooth = (66.0 + 52.0 * jnp.cos(number) + 2.0 * jnp.cos(2.0 * number)) / 120.0
    return number * number, smooth * smooth


def green_table(first, second, third, first_count, second_count, third_count, dtype):
    sq_first, sm_first = wave_terms(first, first_count, dtype)
    sq_second, sm_second = wave_terms(second, second_count, dtype)
    sq_third, sm_third = wave_terms(third, third_count, dtype)
    squared = sq_first + sq_second + sq_third
    nonzero = squared > 0
    safe = jnp.where(nonzero, squared * sm_first * sm_second * sm_third, 1.0)
    return jnp.where(nonzero, COULOMB * jnp.exp(-0.5 * SMEARING * SMEARING * squared) / safe, 0.0)


def reference(atom_frac, atom_charge, cell_x, cell_y, cell_z, tile_count, tile_offset, live_tiles):
    dtype = atom_frac.dtype
    slab_planes = MX // N_GX
    plane_total = slab_planes + 5
    slot_ids = jnp.arange(TILES, dtype=jnp.int32)
    owners = slot_ids // SLOTS
    alive = (slot_ids % SLOTS) < live_tiles[owners]
    counts = jnp.where(alive, tile_count, 0).astype(jnp.int32)
    starts = (owners * slab_planes).astype(jnp.int32)
    fractions = jnp.moveaxis(atom_frac, 1, 0)
    charges = jnp.moveaxis(atom_charge, 1, 0)
    stacked = (fractions, charges, cell_x, cell_y, cell_z, counts, tile_offset, starts)

    def prepare(item):
        fraction, charge, plane_cell, row_cell, column_cell, count, offset, start = item
        row_mask = (jnp.arange(TILE, dtype=jnp.int32) < count).astype(dtype)
        planes = start - 2 + jnp.arange(plane_total, dtype=jnp.int32)
        pairs = tile_factors(fraction, plane_cell + start, row_cell, column_cell, planes)
        plane_index = jnp.remainder(planes, MX).astype(jnp.int32)
        row_index = jnp.remainder(offset + jnp.arange(WIN, dtype=jnp.int32), MY).astype(jnp.int32)
        return charge, row_mask, pairs, plane_index, row_index

    def spread_step(mesh, item):
        charge, row_mask, pairs, plane_index, row_index = prepare(item)
        window = spread_window(charge * row_mask[None], pairs[0], pairs[1], pairs[2])
        return mesh.at[:, plane_index[:, None], row_index[None, :], :].add(window), None

    charge_mesh = lax.scan(spread_step, jnp.zeros((CH, MX, MY, MZ), dtype), stacked)[0]
    green = green_table(jnp.arange(MX, dtype=jnp.int32)[:, None, None], jnp.arange(MY, dtype=jnp.int32)[None, :, None], jnp.arange(MZ, dtype=jnp.int32)[None, None, :], MX, MY, MZ, dtype)
    spectrum = jnp.fft.fftn(charge_mesh, axes=(1, 2, 3))
    potential = jnp.real(jnp.fft.ifftn(spectrum * green[None], axes=(1, 2, 3))).astype(dtype)

    def gather_step(carry, item):
        charge, row_mask, pairs, plane_index, row_index = prepare(item)
        window = potential[:, plane_index[:, None], row_index[None, :], :]
        return carry, gather_window(window, charge, row_mask, pairs[0], pairs[1], pairs[2])

    results = lax.scan(gather_step, jnp.zeros((), jnp.int32), stacked)[1]
    charge_grad = jnp.moveaxis(results[0], 0, 1)
    forces = -jnp.moveaxis(results[1], 0, 1)
    return (charge_grad, forces, potential)
```

```python
import functools
import math

import jax
import jax.numpy as jnp
import numpy as np
from jax import lax
from jax.experimental import pallas as pl
from jax.experimental.pallas import tpu as pltpu
from jax.sharding import PartitionSpec as P

MX = 256
MY = 256
MZ = 256
WIN = 64

SMEARING = 0.7
COULOMB = 8.0

KY_BLOCK = 8
F32 = jnp.float32
BF16 = jnp.bfloat16


def round_up(value, step):
    return -(-value // step) * step


def spline_rows(t):
    t2 = t * t
    t3 = t2 * t
    t4 = t3 * t
    t5 = t4 * t
    rest = 1.0 - t
    r2 = rest * rest
    r4 = r2 * r2
    scale = 1.0 / 120.0
    weights = [
        rest * r4 * scale,
        (26.0 - 50.0 * t + 20.0 * t2 + 20.0 * t3 - 20.0 * t4 + 5.0 * t5) * scale,
        (66.0 - 60.0 * t2 + 30.0 * t4 - 10.0 * t5) * scale,
        (26.0 + 50.0 * t + 20.0 * t2 - 20.0 * t3 - 20.0 * t4 + 10.0 * t5) * scale,
        (1.0 + 5.0 * t + 10.0 * t2 + 10.0 * t3 + 5.0 * t4 - 5.0 * t5) * scale,
        t5 * scale,
    ]
    slopes = [
        -5.0 * r4 * scale,
        (-50.0 + 40.0 * t + 60.0 * t2 - 80.0 * t3 + 25.0 * t4) * scale,
        (-120.0 * t + 120.0 * t3 - 50.0 * t4) * scale,
        (50.0 + 40.0 * t - 60.0 * t2 - 80.0 * t3 + 50.0 * t4) * scale,
        (5.0 + 20.0 * t + 30.0 * t2 + 20.0 * t3 - 25.0 * t4) * scale,
        5.0 * t4 * scale,
    ]
    return weights, slopes


def placed(offsets, rows):
    total = jnp.zeros(offsets.shape, F32)
    for index, row in enumerate(rows):
        total = jnp.where(offsets == index, row, total)
    return total


def halves(value):
    high = value.astype(BF16)
    low = (value - high.astype(F32)).astype(BF16)
    return high, low


def dot(left, right):
    return jnp.dot(left, right, preferred_element_type=F32)


def np_halves(table):
    table = np.asarray(table, np.float32)
    high = table.astype(BF16)
    low = (table - high.astype(np.float32)).astype(BF16)
    return high, low


def cas_np(first, second, count):
    angle = 2.0 * math.pi / count * np.remainder(np.outer(first, second), count)
    return np.cos(angle) + np.sin(angle)


def wave_np(count):
    index = np.arange(count)
    number = 2.0 * math.pi / count * np.where(index < count // 2, index, index - count)
    smooth = (66.0 + 52.0 * np.cos(number) + 2.0 * np.cos(2.0 * number)) / 120.0
    square = number * number
    factor = np.exp(-0.5 * SMEARING * SMEARING * square) / (smooth * smooth) / count
    return square, factor


def factor_kernel(window, live_ref, atoms_ref, table_z_ref, table_y_ref, ez_ref, ezl_ref, ey_ref, bx_ref):
    @pl.when(live_ref[pl.program_id(0)] > 0)
    def _():
        rows = atoms_ref[0]
        tile = rows.shape[1]
        channels = bx_ref.shape[1] // window

        def spread(count, axis, cell, wrap):
            weights, _ = spline_rows(rows[axis : axis + 1])
            cells = rows[cell : cell + 1].astype(jnp.int32)
            index = lax.broadcasted_iota(jnp.int32, (count, tile), 0)
            offsets = (index - cells + 2) & (count - 1) if wrap else index - cells
            return placed(offsets, weights)

        weights_z = spread(MZ, 2, 9, True)
        weights_y = spread(MY, 1, 8, True)
        weights_x = spread(window, 0, 7, False)
        ez = lax.dot_general(
            weights_z,
            table_z_ref[...],
            (((0,), (0,)), ((), ())),
            precision=lax.Precision.HIGHEST,
            preferred_element_type=F32,
        )
        high, low = halves(ez)
        ez_ref[0, :tile] = high
        ez_ref[0, tile:] = high
        ezl_ref[0] = low
        ey_ref[0] = lax.dot_general(
            table_y_ref[...],
            weights_y,
            (((1,), (0,)), ((), ())),
            precision=lax.Precision.HIGHEST,
            preferred_element_type=F32,
        )
        for c in range(channels):
            bx_ref[0, c * window : (c + 1) * window] = weights_x * rows[3 + c : 4 + c]


def solve_kernel(
    geometry,
    live_ref,
    ky_sq_ref,
    ez_ref,
    ezl_ref,
    ey_ref,
    bx_ref,
    fwd_ref,
    back_ref,
    backl_ref,
    inv_ref,
    invl_ref,
    square_ref,
    *rest,
):
    channels, window, block, per_block, group, span, pad = geometry
    outs, (s_ref, y_ref) = rest[:group], rest[group:]
    tiles = ez_ref.shape[0]
    kys = ey_ref.shape[1]
    chunk = pl.program_id(1)
    step = pl.program_id(0)

    @pl.when(chunk == 0)
    def _():
        s_ref[...] = jnp.zeros_like(s_ref)

    def spread_tile(t, carry):
        tile_id = chunk * tiles + t

        @pl.when(live_ref[tile_id] > 0)
        def _():
            start = pl.multiple_of((tile_id // per_block) * block, 8)
            base = bx_ref[t]
            ez = ez_ref[t]
            ezl = ezl_ref[t]
            for k in range(kys):
                high, low = halves(base * ey_ref[t, k : k + 1])
                got = dot(jnp.concatenate([high, low], axis=1), ez) + dot(high, ezl)
                for c in range(channels):
                    s_ref[k, c, pl.ds(start, window)] += got[c * window : (c + 1) * window]

        return carry

    lax.fori_loop(0, tiles, spread_tile, 0)

    @pl.when(chunk == pl.num_programs(1) - 1)
    def _():
        def solve_row(k, carry):
            square = square_ref[...] + ky_sq_ref[step * kys + k]
            recip = jnp.where(square > 0, 1.0 / square, 0.0)
            for c in range(channels):
                s_ref[k, c, : window - block] += s_ref[k, c, MX : MX + window - block]
                high, low = halves(s_ref[k, c, :MX])
                both = dot(fwd_ref[...], high)
                forward = both[:MX] + both[MX:] + dot(fwd_ref[:MX], low)
                high, low = halves(forward * recip)
                y_ref[k, c * group * pad : (c + 1) * group * pad] = (
                    dot(back_ref[...], high) + dot(backl_ref[...], high) + dot(back_ref[...], low)
                )
            return carry

        lax.fori_loop(0, kys, solve_row, 0)
        rows = channels * group * pad
        high, low = halves(y_ref[...].reshape(kys * rows, MZ))
        lines = dot(high, inv_ref[...]) + dot(high, invl_ref[...]) + dot(low, inv_ref[...])
        lines = jnp.swapaxes(lines.reshape(kys, rows, MZ), 0, 1)
        for c in range(channels):
            for m in range(group):
                first = (c * group + m) * pad
                outs[m][c] = lines[first : first + span]


def gather_kernel(group, slab, window_y, scalars_ref, info_ref, table_ref, *rest):
    pieces, (potential_ref, grad_ref, force_ref, plane_ref, wz_ref, wzl_ref, wy_ref, wx_ref) = (
        rest[:group],
        rest[group:],
    )
    c = pl.program_id(0)
    p = pl.program_id(1)
    slots, _, tile = info_ref.shape
    span = wx_ref.shape[2]

    @pl.when((c == 0) & (p == 0))
    def _():
        grad_ref[...] = jnp.zeros_like(grad_ref)
        force_ref[...] = jnp.zeros_like(force_ref)
        for slot in range(slots):
            rows = info_ref[slot]

            def pair(count, axis, cells, wrap):
                weights, slopes = spline_rows(rows[axis : axis + 1])
                index = lax.broadcasted_iota(jnp.int32, (count, tile), 0)
                offsets = index - cells + 2
                offsets = offsets & (count - 1) if wrap else offsets
                return placed(offsets, weights), placed(offsets, slopes)

            cells = rows[7:10].astype(jnp.int32)
            shift = scalars_ref[1 + slot] & 7
            wx_ref[slot, 0], wx_ref[slot, 1] = pair(span, 0, cells[0:1] + 2, False)
            wy_ref[slot, 0], wy_ref[slot, 1] = pair(window_y, 1, cells[1:2] + shift, False)
            for which, value in enumerate(pair(MZ, 2, cells[2:3], True)):
                high, low = halves(value)
                wz_ref[slot, :, which * tile : (which + 1) * tile] = high
                wzl_ref[slot, :, which * tile : (which + 1) * tile] = low

    high, low = halves(jnp.concatenate([piece[0, 0] for piece in pieces], axis=0))
    both = dot(table_ref[...], high)
    plane = both[:MY] + both[MY:] + dot(table_ref[:MY], low)

    @pl.when((p >= 2) & (p < 2 + slab))
    def _():
        potential_ref[0, 0] = plane

    plane_ref[:MY] = plane
    plane_ref[MY:] = plane[:window_y]
    for slot in range(slots):

        @pl.when(slot < scalars_ref[0])
        def _():
            start = pl.multiple_of((scalars_ref[1 + slot] // 8) * 8, 8)
            high, low = halves(plane_ref[pl.ds(start, window_y)])
            got = dot(high, wz_ref[slot]) + dot(high, wzl_ref[slot]) + dot(low, wz_ref[slot])
            summed, slanted = got[:, :tile], got[:, tile:]
            row_sum = jnp.sum(summed * wy_ref[slot, 0], axis=0, keepdims=True)
            row_diff = jnp.sum(summed * wy_ref[slot, 1], axis=0, keepdims=True)
            depth_diff = jnp.sum(slanted * wy_ref[slot, 0], axis=0, keepdims=True)
            mask = info_ref[slot, 10:11]
            weight = wx_ref[slot, 0, pl.ds(p, 1)] * mask
            slope = wx_ref[slot, 1, pl.ds(p, 1)] * mask
            charge = info_ref[slot, pl.ds(3 + c, 1)]
            grad_ref[c, slot : slot + 1] += row_sum * weight
            force_ref[0, slot : slot + 1] -= charge * row_sum * slope
            force_ref[1, slot : slot + 1] -= charge * row_diff * weight
            force_ref[2, slot : slot + 1] -= charge * depth_diff * weight


def on_device(atom_frac, atom_charge, cell_x, cell_y, cell_z, tile_count, tile_offset, live_tiles):
    channels, slots, tile = atom_charge.shape
    devices = lax.axis_size("gx")
    slab = MX // devices
    me = lax.axis_index("gx")
    group = 2 if devices % 2 == 0 else 1
    place = lax.rem(me, group)
    block = max(slab, 16)
    owners = block // slab
    per_block = owners * slots
    window = round_up(block + 5, 8)
    span = slab + 5
    pad = round_up(span, 8)
    kys = MY // group

    slot_ids = jnp.arange(slots, dtype=jnp.int32)
    alive = (slot_ids < live_tiles[0])[:, None]
    mask = (alive & (jnp.arange(tile, dtype=jnp.int32)[None] < tile_count[:, None])).astype(F32)
    fractions = jnp.swapaxes(atom_frac, 0, 1)
    charges = jnp.swapaxes(atom_charge, 0, 1)

    def rows_of(charge, *cells):
        flat = [cell.astype(F32)[:, None] for cell in cells] + [mask[:, None]]
        fill = jnp.zeros((slots, round_up(11, 8) - 4 - len(flat) - channels + 1, tile), F32)
        return jnp.concatenate([fractions, charge] + flat + [fill], axis=1)

    atoms = rows_of(
        charges * mask[:, None],
        cell_x + lax.rem(me, owners) * slab,
        jnp.remainder(cell_y + tile_offset[:, None], MY),
        cell_z,
    )
    info = rows_of(charges, cell_x, cell_y, cell_z)
    everyone = lax.all_gather(atoms, "gx", axis=0, tiled=True)
    tiles = devices * slots
    live = (everyone[:, 10, 0] > 0).astype(jnp.int32)

    square_x, factor_x = wave_np(MX)
    square_y, factor_y = wave_np(MY)
    square_z, factor_z = wave_np(MZ)
    table_x = cas_np(np.arange(MX), np.arange(MX), MX)
    table_y = cas_np(np.arange(MY), np.arange(MY), MY)
    table_z = cas_np(np.arange(MZ), np.arange(MZ), MZ)

    factor_call = pl.pallas_call(
        functools.partial(factor_kernel, window),
        grid_spec=pltpu.PrefetchScalarGridSpec(
            num_scalar_prefetch=1,
            grid=(tiles,),
            in_specs=[
                pl.BlockSpec((1,) + everyone.shape[1:], lambda t, live: (t, 0, 0)),
                pl.BlockSpec((MZ, MZ), lambda t, live: (0, 0)),
                pl.BlockSpec((kys, MY), lambda t, live: (0, 0)),
            ],
            out_specs=[
                pl.BlockSpec((1, 2 * tile, MZ), lambda t, live: (t, 0, 0)),
                pl.BlockSpec((1, tile, MZ), lambda t, live: (t, 0, 0)),
                pl.BlockSpec((1, kys, tile), lambda t, live: (t, 0, 0)),
                pl.BlockSpec((1, channels * window, tile), lambda t, live: (t, 0, 0)),
            ],
        ),
        out_shape=[
            jax.ShapeDtypeStruct((tiles, 2 * tile, MZ), BF16),
            jax.ShapeDtypeStruct((tiles, tile, MZ), BF16),
            jax.ShapeDtypeStruct((tiles, kys, tile), F32),
            jax.ShapeDtypeStruct((tiles, channels * window, tile), F32),
        ],
        name="factors",
    )
    own_y = lax.dynamic_slice_in_dim(
        jnp.asarray(table_y * factor_y[:, None] * COULOMB, F32), place * kys, kys, 0
    )
    ez, ezl, ey, bx = factor_call(live, everyone, jnp.asarray(table_z * factor_z[None], F32), own_y)

    ky_sq = lax.dynamic_slice_in_dim(jnp.asarray(square_y, F32), place * kys, kys, 0)
    forward = cas_np(np.arange(MX), np.arange(MX) - 2, MX) * factor_x[:, None]
    forward = np.concatenate(np_halves(forward), axis=0)
    members = [me - place + lax.rem(place + m, group) for m in range(group)]
    back_high, back_low = np_halves(table_x)

    def plane_rows(table):
        wrapped = jnp.asarray(np.concatenate([table, table[:pad]], axis=0))
        rows = [
            lax.dynamic_slice_in_dim(wrapped, jnp.remainder(member * slab - 2, MX), pad, 0)
            for member in members
        ]
        return jnp.concatenate(rows, axis=0)

    inv_high, inv_low = np_halves(table_z)
    chunk = min(tiles, 32)
    geometry = (channels, window, block, per_block, group, span, pad)
    whole = lambda *shape: pl.BlockSpec(shape, lambda k, t, *_: (0,) * len(shape))
    pieces = pl.pallas_call(
        functools.partial(solve_kernel, geometry),
        grid_spec=pltpu.PrefetchScalarGridSpec(
            num_scalar_prefetch=2,
            grid=(kys // KY_BLOCK, tiles // chunk),
            in_specs=[
                pl.BlockSpec((chunk, 2 * tile, MZ), lambda k, t, *_: (t, 0, 0)),
                pl.BlockSpec((chunk, tile, MZ), lambda k, t, *_: (t, 0, 0)),
                pl.BlockSpec((chunk, KY_BLOCK, tile), lambda k, t, *_: (t, k, 0)),
                pl.BlockSpec((chunk, channels * window, tile), lambda k, t, *_: (t, 0, 0)),
                whole(2 * MX, MX),
                whole(group * pad, MX),
                whole(group * pad, MX),
                whole(MZ, MZ),
                whole(MZ, MZ),
                whole(MX, MZ),
            ],
            out_specs=[
                pl.BlockSpec((channels, span, KY_BLOCK, MZ), lambda k, t, *_: (0, 0, k, 0))
            ]
            * group,
            scratch_shapes=[
                pltpu.VMEM((KY_BLOCK, channels, MX + window - block, MZ), F32),
                pltpu.VMEM((KY_BLOCK, channels * group * pad, MZ), F32),
            ],
        ),
        out_shape=[jax.ShapeDtypeStruct((channels, span, kys, MZ), F32)] * group,
        name="solve",
    )(
        live,
        ky_sq,
        ez,
        ezl,
        ey,
        bx,
        jnp.asarray(forward),
        plane_rows(back_high),
        plane_rows(back_low),
        jnp.asarray(inv_high),
        jnp.asarray(inv_low),
        jnp.asarray(square_x[:, None] + square_z[None], F32),
    )

    arrived = [pieces[0]]
    for m in range(1, group):
        route = [(i, i - i % group + (i % group + m) % group) for i in range(devices)]
        arrived.append(lax.ppermute(pieces[m], "gx", route))
    inverse_y = np.concatenate(np_halves(table_y), axis=0)
    columns = [
        lax.dynamic_slice_in_dim(
            jnp.asarray(inverse_y), lax.rem(place - m + group, group) * kys, kys, 1
        )
        for m in range(group)
    ]
    window_y = WIN + 8
    scalars = jnp.concatenate([live_tiles, tile_offset])
    potential, charge_grad, forces = pl.pallas_call(
        functools.partial(gather_kernel, group, slab, window_y),
        grid_spec=pltpu.PrefetchScalarGridSpec(
            num_scalar_prefetch=1,
            grid=(channels, span),
            in_specs=[
                pl.BlockSpec(info.shape, lambda c, p, s: (0, 0, 0)),
                pl.BlockSpec((2 * MY, MY), lambda c, p, s: (0, 0)),
            ]
            + [pl.BlockSpec((1, 1, kys, MZ), lambda c, p, s: (c, p, 0, 0))] * group,
            out_specs=[
                pl.BlockSpec(
                    (1, 1, MY, MZ), lambda c, p, s: (c, jnp.clip(p - 2, 0, slab - 1), 0, 0)
                ),
                pl.BlockSpec((channels, slots, tile), lambda c, p, s: (0, 0, 0)),
                pl.BlockSpec((3, slots, tile), lambda c, p, s: (0, 0, 0)),
            ],
            scratch_shapes=[
                pltpu.VMEM((MY + window_y, MZ), F32),
                pltpu.VMEM((slots, MZ, 2 * tile), BF16),
                pltpu.VMEM((slots, MZ, 2 * tile), BF16),
                pltpu.VMEM((slots, 2, window_y, tile), F32),
                pltpu.VMEM((slots, 2, span, tile), F32),
            ],
        ),
        out_shape=[
            jax.ShapeDtypeStruct((channels, slab, MY, MZ), F32),
            jax.ShapeDtypeStruct((channels, slots, tile), F32),
            jax.ShapeDtypeStruct((3, slots, tile), F32),
        ],
        name="gather",
    )(scalars, info, jnp.concatenate(columns, axis=1), *arrived)
    return (charge_grad, forces, potential)


def solution(mesh):
    in_specs = (
        P(None, ("box", "gx"), None),
        P(None, ("box", "gx"), None),
        P(("box", "gx"), None),
        P(("box", "gx"), None),
        P(("box", "gx"), None),
        P(("box", "gx")),
        P(("box", "gx")),
        P(("box", "gx")),
    )
    out_specs = (
        P(None, ("box", "gx"), None),
        P(None, ("box", "gx"), None),
        P(None, ("box", "gx"), None, None),
    )
    return jax.shard_map(
        on_device, mesh=mesh, in_specs=in_specs, out_specs=out_specs, check_vma=False
    )
```
